32 devices in a mesh: bead: 4 (over x, core), slab: 8 (over z, y).
Axes of the slice: x: 2, y: 2, z: 4, core: 2. Of those that a mesh axis runs over, the one named last changes fastest.
Arguments:
- positions: float32 [16, 3, 8192], P('bead', None, 'slab'), may hold values from -0.4 to 16.4, as said below
- velocities: float32 [16, 3, 8192], P('bead', None, 'slab'), may hold values from -5 to 5
- masses: float32 [8192], P('slab'), may hold values from 1 to 16
- amplitudes: float32 [8192], P('slab'), may hold values from 0.15 to 0.6
- charges: float32 [8192], P('slab'), may hold values from -1.2 to 1.2
Outputs:
- moved: float32 [16, 3, 8192], P('bead', None, 'slab')
- final_velocities: float32 [16, 3, 8192], P('bead', None, 'slab')
The draws below stay inside these ranges and needn't reach their ends.
Inputs may be any that keep to these rules, and one draw needn't show every extreme that they name: `positions`: atom n's beads lie within 0.4 of its cell: plane n // 512 spans first coordinates from its index to its index plus one, and cell (n % 512) // 128 = 2 a + e of that plane spans second coordinates a to a + 1 and third coordinates e to e + 1.
All inputs are finite; a program needn't handle non-finite values.
Results may differ from the reference program's by a relative error of at most 0.0003.
Values sent between devices are 32-bit elements; how exact they have to be, the bound alone decides.
A program may use at most 64 MiB of HBM per device.

```python
import math
import jax
import jax.numpy as jnp
from jax import lax

CELL_ATOMS = 128
INNER_STEPS = 2
OUTER_STEPS = 2
PLANE_ATOMS = 512
BEADS = 16
CBEADS = 4
ATOMS = 8192


def draw_positions(key, part):
    first_key = jax.random.fold_in(key, 11)
    second_key = jax.random.fold_in(key, 23)
    third_key = jax.random.fold_in(key, 37)
    fourth_key = jax.random.fold_in(key, 41)
    index = jnp.arange(ATOMS, dtype=jnp.int32)
    plane = (index // PLANE_ATOMS).astype(jnp.float32)
    cell = index % PLANE_ATOMS // CELL_ATOMS
    corner = jnp.stack([plane, (cell // 2).astype(jnp.float32), (cell % 2).astype(jnp.float32)])
    centre = corner + jax.random.uniform(first_key, (3, ATOMS), jnp.float32)
    mode_count = CBEADS // 2 - 1
    modes = jnp.arange(1, mode_count + 1, dtype=jnp.float32)
    cycle_place = 2.0 * jnp.pi * jnp.arange(BEADS, dtype=jnp.float32) / BEADS
    angle = modes[:, None] * cycle_place[None, :]
    cosine = jnp.cos(angle)
    sine = jnp.sin(angle)
    factor = 0.15
    cos_coef = factor * jax.random.normal(second_key, (mode_count, 3, ATOMS), jnp.float32)
    sin_coef = factor * jax.random.normal(third_key, (mode_count, 3, ATOMS), jnp.float32)
    rough = jax.random.uniform(fourth_key, (BEADS, 3, ATOMS), jnp.float32, -0.08, 0.08)
    smooth = jnp.einsum('kb,kca->bca', cosine, cos_coef, precision=lax.Precision.HIGHEST)
    smooth = smooth + jnp.einsum('kb,kca->bca', sine, sin_coef, precision=lax.Precision.HIGHEST)
    spread = 0.3 * jnp.tanh(smooth / 0.3) + rough
    return centre[None] + spread


def level_of(own_key, shape, pieces, low, largest):
    def one(position, blocks):
        draws = jax.random.uniform(jax.random.fold_in(jax.random.fold_in(own_key, 6), position), (blocks,), jnp.float32, low / len(pieces), largest / len(pieces))
        return jnp.repeat(jnp.exp(draws), shape[position] // blocks).reshape((-1,) + (1,) * (len(shape) - position - 1))

    loudness = one(*pieces[0])
    for cut in pieces[1:]:
        loudness = loudness * one(*cut)
    return loudness


def gaussian(own_key, shape, scale, most, shards=(), kind=jnp.bfloat16):
    array = scale * jax.random.normal(own_key, shape, jnp.float32)
    if shards:
        array = array * level_of(own_key, shape, shards, -0.22, 0.18)
    return jnp.clip(array, -most, most).astype(kind)


def setup_inputs(seed: int = 0) -> dict:
    splits = jax.random.split(jax.random.key(seed), 6)
    positions = draw_positions(jax.random.fold_in(splits[5], 71), 0)
    velocities = gaussian(splits[1], (BEADS, 3, ATOMS), 1.0, 5.0, ((0, 4), (2, 8)), jnp.float32)
    masses = jnp.clip(jnp.exp(math.log(16.0) - 2.7725887 * jax.random.uniform(splits[2], (ATOMS,), jnp.float32) ** level_of(splits[2], (ATOMS,), ((0, 8),), -0.2, 0.2)), 1.0, 16.0)
    amplitudes = jnp.clip(jnp.exp(math.log(0.6) - 1.3862944 * jax.random.uniform(splits[3], (ATOMS,), jnp.float32) ** level_of(splits[3], (ATOMS,), ((0, 8),), -0.2, 0.2)), 0.15, 0.6)
    charges = jnp.clip(jax.random.uniform(splits[4], (ATOMS,), jnp.float32, -1.2, 1.2) * level_of(splits[4], (ATOMS,), ((0, 8),), -0.4, 0.0), -1.2, 1.2)
    return {"positions": positions, "velocities": velocities, "masses": masses, "amplitudes": amplitudes, "charges": charges}


time_step = 0.05
spring_rate = 25.0
near_scale = 4.0
far_scale = 2.0


def contraction(bead_count, small_count):
    bead_place = jnp.arange(bead_count, dtype=jnp.float32) / bead_count
    small_place = jnp.arange(small_count, dtype=jnp.float32) / small_count
    phase = 2.0 * jnp.pi * (bead_place[None, :] - small_place[:, None])
    modes = jnp.arange(1, small_count // 2, dtype=jnp.float32)
    total = 1.0 + jnp.cos(0.5 * small_count * phase) + 2.0 * jnp.sum(jnp.cos(modes[:, None, None] * phase[None]), axis=0)
    return total / bead_count


def pair_force(targets, sources, target_share, source_share, scale):
    between = targets[..., :, :, None] - sources[..., :, None, :]
    square = jnp.sum(between * between, axis=-3)
    weight = target_share[:, None] * source_share[None, :] * jnp.exp(-0.5 * scale * square) * scale
    return jnp.sum(weight[..., None, :, :] * between, axis=-1)


def field_forces(coords, shares, reach, scale):
    plane_size = PLANE_ATOMS
    planes_total = ATOMS // PLANE_ATOMS
    margin = reach * plane_size
    offset = jnp.concatenate([jnp.full((margin,), -float(planes_total), jnp.float32), jnp.zeros((ATOMS,), jnp.float32), jnp.full((margin,), float(planes_total), jnp.float32)])
    shift = jnp.stack([offset, jnp.zeros_like(offset), jnp.zeros_like(offset)])
    extended = jnp.concatenate([coords[..., -margin:], coords, coords[..., :margin]], axis=-1) + shift
    shares_wide = jnp.concatenate([shares[-margin:], shares, shares[:margin]])
    width = (2 * reach + 1) * plane_size

    def one_plane(plane):
        start = plane * plane_size
        targets = lax.dynamic_slice_in_dim(coords, start, plane_size, 2)
        sources = lax.dynamic_slice_in_dim(extended, start, width, 2)
        target_share = lax.dynamic_slice_in_dim(shares, start, plane_size, 0)
        source_share = lax.dynamic_slice_in_dim(shares_wide, start, width, 0)
        return pair_force(targets, sources, target_share, source_share, scale)

    forces = lax.map(one_plane, jnp.arange(planes_total, dtype=jnp.int32))
    return jnp.transpose(forces, (1, 2, 0, 3)).reshape(coords.shape)


def reference(positions, velocities, masses, amplitudes, charges):
    table = contraction(BEADS, CBEADS)

    def fast(coords):
        springs = 2.0 * coords - jnp.roll(coords, 1, 0) - jnp.roll(coords, -1, 0)
        return field_forces(coords, amplitudes, 1, near_scale) - spring_rate * masses * springs

    def slow(coords):
        contracted = jnp.einsum("cb,bka->cka", table, coords, precision=lax.Precision.HIGHEST)
        far = field_forces(contracted, charges, 2, far_scale)
        return (BEADS / CBEADS) * jnp.einsum("cb,cka->bka", table, far, precision=lax.Precision.HIGHEST)

    inverse = 1.0 / masses
    outer_dt = INNER_STEPS * time_step
    coords = positions
    speeds = velocities
    quick = fast(coords)
    gentle = slow(coords)
    for outer_step in range(OUTER_STEPS):
        speeds = speeds + 0.5 * outer_dt * gentle * inverse
        for inner_step in range(INNER_STEPS):
            speeds = speeds + 0.5 * time_step * quick * inverse
            coords = coords + time_step * speeds
            quick = fast(coords)
            speeds = speeds + 0.5 * time_step * quick * inverse
        gentle = slow(coords)
        speeds = speeds + 0.5 * outer_dt * gentle * inverse
    return coords - positions, speeds
```

```python
import math

import jax
import jax.numpy as jnp
import numpy as np
from jax import lax
from jax.experimental import pallas as pl
from jax.experimental.pallas import tpu as pltpu
from jax.sharding import PartitionSpec as P

INNER_STEPS = 2
OUTER_STEPS = 2
PLANE_ATOMS = 512

time_step = 0.05
spring_rate = 25.0
near_scale = 4.0
far_scale = 2.0

MESH = pl.DeviceIdType.MESH
F32 = jnp.float32
BF16 = jnp.bfloat16
PA = PLANE_ATOMS
PHASES = INNER_STEPS * OUTER_STEPS + 1
EVENTS = OUTER_STEPS + 1
FEATURES = 64


def contraction(bead_count, small_count):
    bead_place = np.arange(bead_count, dtype=np.float64) / bead_count
    small_place = np.arange(small_count, dtype=np.float64) / small_count
    phase = 2.0 * np.pi * (bead_place[None, :] - small_place[:, None])
    modes = np.arange(1, small_count // 2, dtype=np.float64)
    total = 1.0 + np.cos(0.5 * small_count * phase)
    total = total + 2.0 * np.sum(np.cos(modes[:, None, None] * phase[None]), axis=0)
    return (total / bead_count).astype(np.float32)


def rows_of(width):
    return lax.broadcasted_iota(jnp.int32, (8, width), 0)


def cut(x):
    high = x.astype(BF16).astype(F32)
    rest = x - high
    mid = rest.astype(BF16).astype(F32)
    low = (rest - mid).astype(BF16).astype(F32)
    return high, mid, low


def scaled(x, first_centre, rate):
    quarter = rows_of(x.shape[1]) & 3
    centre = jnp.where(quarter == 0, first_centre, jnp.where(quarter == 3, 0.0, 1.0))
    return (x - centre) * rate


def source_features(z, share):
    quarter = rows_of(z.shape[1]) & 3
    square = 0.5 * z * z
    norm = pltpu.roll(square, 1, 0) + pltpu.roll(square, 2, 0) + pltpu.roll(square, 3, 0)
    high, mid, low = cut(jnp.where(quarter == 3, norm, z))
    one = jnp.ones_like(z)
    features = jnp.concatenate([high, high, mid, mid, high, low, one, jnp.zeros_like(z)], axis=0)
    weighted = share * jnp.where(quarter == 3, 1.0, z)
    first, second, _ = cut(weighted)
    return features.T.astype(BF16), jnp.concatenate([first, second], axis=0).astype(BF16)


def target_features(z):
    quarter = rows_of(z.shape[1]) & 3
    square = 0.5 * z * z
    norm = pltpu.roll(square, 1, 0) + pltpu.roll(square, 2, 0) + pltpu.roll(square, 3, 0)
    high, mid, low = cut(jnp.where(quarter == 3, norm, z))
    flat = quarter == 3
    own = jnp.where(
        flat,
        -high,
        jnp.where(quarter == 2, -pltpu.roll(mid, 7, 0), jnp.where(quarter == 1, -pltpu.roll(low, 6, 0), 0.0)),
    )
    high = jnp.where(flat, -1.0, high)
    mid = jnp.where(flat, 0.0, mid)
    low = jnp.where(flat, 0.0, low)
    return [high, mid, high, mid, low, high, own, jnp.zeros_like(z)]


def masked(groups, half):
    keep = (rows_of(groups[0].shape[1]) >> 2) == half
    return jnp.concatenate([jnp.where(keep, g, 0.0) for g in groups], axis=0).astype(BF16)


def block_sums(sources, weighted, targets, pieces):
    weight = jnp.exp2(jnp.dot(sources, targets, preferred_element_type=F32))
    high = weight.astype(BF16)
    total = jnp.dot(weighted, high, preferred_element_type=F32)
    if pieces == 2:
        rest = (weight - high.astype(F32)).astype(BF16)
        total = total + jnp.dot(weighted, rest, preferred_element_type=F32)
    return total


def forces_of(z, sums):
    quarter = rows_of(z.shape[1]) & 3
    plain = jnp.where(quarter == 3, sums, 0.0)
    spread = pltpu.roll(plain, 7, 0) + pltpu.roll(plain, 6, 0) + pltpu.roll(plain, 5, 0)
    return jnp.where(quarter == 3, 0.0, z * spread - sums)


def kernel(
    nb, ns, planes_total,
    table, pos, vel, mass, amp, chg,
    moved, final,
    X, V, AF, AS, prm, prm_l, prm_r, halo_l, halo_r, ring_p, ring_n,
    part_s, part_r, Y, y_l, y_r, far_s, far_r,
    nST, nXS, nT, nG, fST, fXS, fT, fG,
    prm_ss, prm_rs, halo_ss, halo_rs, ring_ss, ring_rs, part_ss, part_rs, y_ss, y_rs, far_ss, far_rs,
):
    me_b = lax.axis_index("bead")
    me_s = lax.axis_index("slab")
    left = (me_b, lax.rem(me_s + ns - 1, ns))
    right = (me_b, lax.rem(me_s + 1, ns))
    prev = (lax.rem(me_b + nb - 1, nb), me_s)
    after = (lax.rem(me_b + 1, nb), me_s)
    pairs = X.shape[1]
    beads_here = 2 * pairs
    atoms = X.shape[3]
    first_bead = me_b * beads_here

    def remote(src, dst, ss, rs, to):
        return pltpu.make_async_remote_copy(
            src_ref=src, dst_ref=dst, send_sem=ss, recv_sem=rs, device_id=to, device_id_type=MESH
        )

    barrier = pltpu.get_barrier_semaphore()
    pl.semaphore_signal(barrier, inc=1, device_id=left, device_id_type=MESH)
    pl.semaphore_signal(barrier, inc=1, device_id=right, device_id_type=MESH)
    for d in range(1, nb):
        other = (lax.rem(me_b + d, nb), me_s)
        pl.semaphore_signal(barrier, inc=1, device_id=other, device_id_type=MESH)

    X[0] = jnp.zeros((pairs, 8, atoms), F32)
    V[...] = jnp.zeros_like(V)
    for b in range(beads_here):
        p, r = b // 2, 4 * (b % 2)
        X[0, p, r:r + 3, :] = pos[b]
        V[p, r:r + 3, :] = vel[b]
    prm[...] = jnp.zeros_like(prm)
    for t in range(2):
        lanes = slice(t * PA, (t + 1) * PA)
        prm[t:t + 1, :] = amp[:, lanes]
        prm[2 + t:3 + t, :] = chg[:, lanes]

    pl.semaphore_wait(barrier, nb + 1)

    prm_copies = [
        remote(prm, prm_r, prm_ss.at[0], prm_rs.at[0], left),
        remote(prm, prm_l, prm_ss.at[1], prm_rs.at[1], right),
    ]
    for copy in prm_copies:
        copy.start()

    centre = (me_s * 2).astype(F32) + 1.0
    span = float(planes_total)
    centre_l = centre + jnp.where(me_s == 0, span, 0.0)
    centre_r = centre - jnp.where(me_s == ns - 1, span, 0.0)
    near_rate = math.sqrt(near_scale / math.log(2.0))
    far_rate = math.sqrt(far_scale / math.log(2.0))

    inverse = 1.0 / mass[...]

    def halo_copies(k):
        return [
            remote(X.at[k, :, :, pl.ds(0, PA)], halo_r.at[k], halo_ss.at[k, 0], halo_rs.at[k, 0], left),
            remote(X.at[k, :, :, pl.ds(atoms - PA, PA)], halo_l.at[k], halo_ss.at[k, 1], halo_rs.at[k, 1], right),
        ]

    def ring_copies(k):
        return [
            remote(X.at[k, pairs - 1], ring_p.at[k], ring_ss.at[k, 0], ring_rs.at[k, 0], after),
            remote(X.at[k, 0], ring_n.at[k], ring_ss.at[k, 1], ring_rs.at[k, 1], prev),
        ]

    def spoke_copies(src, dst, ss, rs, e):
        return [
            remote(src(d), dst.at[e, d], ss.at[e, d], rs.at[e, d], (lax.rem(me_b + d, nb), me_s))
            for d in range(1, nb)
        ]

    def part_copies(e):
        return spoke_copies(lambda d: part_s.at[e, d], part_r, part_ss, part_rs, e)

    def far_copies(e):
        return spoke_copies(lambda d: far_s.at[e], far_r, far_ss, far_rs, e)

    def y_copies(e):
        return [
            remote(Y.at[e], y_r.at[e], y_ss.at[e, 0], y_rs.at[e, 0], left),
            remote(Y.at[e], y_l.at[e], y_ss.at[e, 1], y_rs.at[e, 1], right),
        ]

    low_rows = rows_of(PA) < 4

    def partial_of(k, c):
        total = None
        for p in range(pairs):
            first = table[c, first_bead + 2 * p]
            second = table[c, first_bead + 2 * p + 1]
            term = jnp.where(rows_of(atoms) < 4, first, second) * X[k, p]
            total = term if total is None else total + term
        total = total + pltpu.roll(total, 4, 0)
        return jnp.where(low_rows, total[:, :PA], total[:, PA:])

    def far_halves(tile):
        first = jnp.where(low_rows, tile, 0.0)
        second = jnp.where(low_rows, pltpu.roll(tile, 4, 0), 0.0)
        return first, second

    def near_block(p, t, q):
        sources, weighted = nST[p, q], nXS[p, q]
        first = block_sums(sources, weighted, nT[p, t, 0], 1)
        second = block_sums(sources, weighted, nT[p, t, 1], 1)
        both = jnp.where(low_rows, first[:8] + first[8:], second[:8] + second[8:])
        nG[p, t] += both

    def far_block(t, q):
        sums = block_sums(fST[q], fXS[q], fT[t], 2)
        fG[t] += sums[:8] + sums[8:]

    def phase(k, carry):
        slow_turn = lax.rem(k, INNER_STEPS) == 0
        e = k // INNER_STEPS
        for copy in halo_copies(k):
            copy.start()

        @pl.when(slow_turn)
        def _():
            for d in range(1, nb):
                part_s[e, d] = partial_of(k, lax.rem(me_b + d, nb))
            for copy in part_copies(e):
                copy.start()

        for copy in ring_copies(k):
            copy.start()

        for p in range(pairs):
            for t in range(2):
                lanes = slice(t * PA, (t + 1) * PA)
                z = scaled(X[k, p, :, lanes], centre, near_rate)
                nST[p, 1 + t], nXS[p, 1 + t] = source_features(z, amp[:, lanes])
                groups = target_features(z)
                nT[p, t, 0] = masked(groups, 0)
                nT[p, t, 1] = masked(groups, 1)
        nG[...] = jnp.zeros_like(nG)

        @pl.loop(0, pairs * 2)
        def _(n):
            p, t = n // 2, lax.rem(n, 2)
            near_block(p, t, 1)
            near_block(p, t, 2)

        @pl.when(k == 0)
        def _():
            for copy in prm_copies:
                copy.wait_recv()

        @pl.when(slow_turn)
        def _():
            total = partial_of(k, me_b)
            for d, copy in enumerate(part_copies(e)):
                copy.wait_recv()
                total = total + part_r[e, d + 1]
            Y[e] = total
            for copy in y_copies(e):
                copy.start()
            for t, half in enumerate(far_halves(total)):
                z = scaled(half, centre, far_rate)
                z = jnp.where(low_rows, z, 0.0)
                fST[2 + t], fXS[2 + t] = source_features(z, chg[:, t * PA:(t + 1) * PA])
                fT[t] = masked(target_features(z), 0)
            fG[...] = jnp.zeros_like(fG)

            @pl.loop(0, 2)
            def _(t):
                far_block(t, 2)
                far_block(t, 3)

            for copy in y_copies(e):
                copy.wait_recv()
            for base, tile, shares, middle in ((0, y_l, prm_l, centre_l), (4, y_r, prm_r, centre_r)):
                for t, half in enumerate(far_halves(tile[e])):
                    z = scaled(half, middle, far_rate)
                    z = jnp.where(low_rows, z, 0.0)
                    fST[base + t], fXS[base + t] = source_features(z, shares[2 + t:3 + t, :])

            @pl.loop(0, 2)
            def _(t):
                far_block(t, 1)
                far_block(t, 4)
                far_block(t, 5 * t)

            halves = []
            for t in range(2):
                lanes = slice(t * PA, (t + 1) * PA)
                z = scaled(far_halves(total)[t], centre, far_rate)
                coefficient = chg[:, lanes] * (far_scale / far_rate)
                halves.append(coefficient * forces_of(z, fG[t]))
            far_s[e] = jnp.where(low_rows, halves[0], pltpu.roll(halves[1], 4, 0))
            for copy in far_copies(e):
                copy.start()

        for copy in halo_copies(k):
            copy.wait_recv()
        for p in range(pairs):
            z = scaled(halo_l[k, p], centre_l, near_rate)
            nST[p, 0], nXS[p, 0] = source_features(z, prm_l[1:2, :])
            z = scaled(halo_r[k, p], centre_r, near_rate)
            nST[p, 3], nXS[p, 3] = source_features(z, prm_r[0:1, :])

        @pl.loop(0, pairs)
        def _(p):
            near_block(p, 0, 0)
            near_block(p, 1, 3)

        for copy in ring_copies(k):
            copy.wait_recv()
        upper = rows_of(atoms) < 4
        rolled = [pltpu.roll(X[k, p], 4, 0) for p in range(pairs)]
        before = [pltpu.roll(ring_p[k], 4, 0)] + rolled
        behind = rolled + [pltpu.roll(ring_n[k], 4, 0)]
        for p in range(pairs):
            springs = 2.0 * X[k, p] - rolled[p] - jnp.where(upper, before[p], behind[p + 1])
            AF[p] = -spring_rate * springs
            for t in range(2):
                lanes = slice(t * PA, (t + 1) * PA)
                z = scaled(X[k, p, :, lanes], centre, near_rate)
                coefficient = amp[:, lanes] * (near_scale / near_rate) * inverse[:, lanes]
                AF[p, :, lanes] += coefficient * forces_of(z, nG[p, t])

        edge = (k == 0) | (k == PHASES - 1)
        fast_step = jnp.where(edge, 0.5 * time_step, time_step)
        slow_step = jnp.where(edge, 0.5 * INNER_STEPS * time_step, INNER_STEPS * time_step)
        for p in range(pairs):
            V[p] += fast_step * AF[p]

        @pl.when(slow_turn)
        def _():
            for copy in far_copies(e):
                copy.wait_recv()
            ratio = float(beads_here)
            total = [[None, None] for _ in range(pairs)]
            for d in range(nb):
                tile = far_s[e] if d == 0 else far_r[e, d]
                c = lax.rem(me_b + nb - d, nb)
                turned = pltpu.roll(tile, 4, 0)
                doubled = (jnp.where(low_rows, tile, turned), jnp.where(low_rows, turned, tile))
                for p in range(pairs):
                    first = table[c, first_bead + 2 * p] * ratio
                    second = table[c, first_bead + 2 * p + 1] * ratio
                    level = jnp.where(low_rows, first, second)
                    for t in range(2):
                        term = level * doubled[t]
                        total[p][t] = term if d == 0 else total[p][t] + term
            for p in range(pairs):
                for t in range(2):
                    lanes = slice(t * PA, (t + 1) * PA)
                    V[p, :, lanes] += slow_step * inverse[:, lanes] * total[p][t]

        @pl.when(k < PHASES - 1)
        def _():
            for p in range(pairs):
                X[k + 1, p] = X[k, p] + time_step * V[p]

        return carry

    lax.fori_loop(0, PHASES, phase, 0)

    last = PHASES - 1
    for b in range(beads_here):
        p, r = b // 2, 4 * (b % 2)
        moved[b] = X[last, p, r:r + 3, :] - pos[b]
        final[b] = V[p, r:r + 3, :]

    for copy in prm_copies:
        copy.wait_send()

    @pl.loop(0, PHASES)
    def _(k):
        for copy in halo_copies(k) + ring_copies(k):
            copy.wait_send()

    @pl.loop(0, EVENTS)
    def _(e):
        for copy in part_copies(e) + y_copies(e) + far_copies(e):
            copy.wait_send()


def solution(mesh):
    nb, ns = mesh.shape["bead"], mesh.shape["slab"]

    def shards(positions, velocities, masses, amplitudes, charges):
        beads_here, _, atoms = positions.shape
        assert atoms == 2 * PA and beads_here % 2 == 0
        pairs = beads_here // 2
        table = jnp.asarray(contraction(beads_here * nb, nb))
        vmem = pl.BlockSpec(memory_space=pltpu.VMEM)
        out = jax.ShapeDtypeStruct(positions.shape, F32)
        V, D = pltpu.VMEM, pltpu.SemaphoreType.DMA
        tile = (8, PA)

        def body(*refs):
            kernel(nb, ns, 2 * ns, *refs)

        return pl.pallas_call(
            body,
            name="rod",
            out_shape=(out, out),
            in_specs=[pl.BlockSpec(memory_space=pltpu.SMEM)] + [vmem] * 5,
            out_specs=(vmem, vmem),
            scratch_shapes=[
                V((PHASES, pairs, 8, atoms), F32),
                V((pairs, 8, atoms), F32),
                V((pairs, 8, atoms), F32),
                V((pairs, 8, atoms), F32),
                V(tile, F32), V(tile, F32), V(tile, F32),
                V((PHASES, pairs) + tile, F32), V((PHASES, pairs) + tile, F32),
                V((PHASES, 8, atoms), F32), V((PHASES, 8, atoms), F32),
                V((EVENTS, nb) + tile, F32), V((EVENTS, nb) + tile, F32),
                V((EVENTS,) + tile, F32), V((EVENTS,) + tile, F32), V((EVENTS,) + tile, F32),
                V((EVENTS,) + tile, F32), V((EVENTS, nb) + tile, F32),
                V((pairs, 4, PA, FEATURES), BF16), V((pairs, 4, 16, PA), BF16),
                V((pairs, 2, 2, FEATURES, PA), BF16), V((pairs, 2) + tile, F32),
                V((6, PA, FEATURES), BF16), V((6, 16, PA), BF16),
                V((2, FEATURES, PA), BF16), V((2,) + tile, F32),
                D((2,)), D((2,)), D((PHASES, 2)), D((PHASES, 2)), D((PHASES, 2)), D((PHASES, 2)),
                D((EVENTS, nb)), D((EVENTS, nb)), D((EVENTS, 2)), D((EVENTS, 2)),
                D((EVENTS, nb)), D((EVENTS, nb)),
            ],
            compiler_params=pltpu.CompilerParams(collective_id=0, has_side_effects=True),
        )(table, positions, velocities, masses[None], amplitudes[None], charges[None])

    both = P("bead", None, "slab")
    return jax.shard_map(
        shards, mesh=mesh, in_specs=(both, both, P("slab"), P("slab"), P("slab")), out_specs=(both, both), check_vma=False
    )
```

```python
import math

import jax
import jax.numpy as jnp
import numpy as np
from jax import lax
from jax.experimental import pallas as pl
from jax.experimental.pallas import tpu as pltpu
from jax.sharding import PartitionSpec as P

INNER_STEPS = 2
OUTER_STEPS = 2
PLANE_ATOMS = 512

time_step = 0.05
spring_rate = 25.0
near_scale = 4.0
far_scale = 2.0

MESH = pl.DeviceIdType.MESH
F32 = jnp.float32
BF16 = jnp.bfloat16
PA = PLANE_ATOMS
PHASES = INNER_STEPS * OUTER_STEPS + 1
EVENTS = OUTER_STEPS + 1
FEATURES = 64
HALF = PA // 2


def contraction(bead_count, small_count):
    bead_place = np.arange(bead_count, dtype=np.float64) / bead_count
    small_place = np.arange(small_count, dtype=np.float64) / small_count
    phase = 2.0 * np.pi * (bead_place[None, :] - small_place[:, None])
    modes = np.arange(1, small_count // 2, dtype=np.float64)
    total = 1.0 + np.cos(0.5 * small_count * phase)
    total = total + 2.0 * np.sum(np.cos(modes[:, None, None] * phase[None]), axis=0)
    return (total / bead_count).astype(np.float32)


def rows_of(width):
    return lax.broadcasted_iota(jnp.int32, (8, width), 0)


def cut(x):
    high = x.astype(BF16).astype(F32)
    rest = x - high
    mid = rest.astype(BF16).astype(F32)
    low = (rest - mid).astype(BF16).astype(F32)
    return high, mid, low


def scaled(x, first_centre, rate):
    quarter = rows_of(x.shape[1]) & 3
    centre = jnp.where(quarter == 0, first_centre, jnp.where(quarter == 3, 0.0, 1.0))
    return (x - centre) * rate


def source_features(z, share):
    quarter = rows_of(z.shape[1]) & 3
    square = 0.5 * z * z
    norm = pltpu.roll(square, 1, 0) + pltpu.roll(square, 2, 0) + pltpu.roll(square, 3, 0)
    high, mid, low = cut(jnp.where(quarter == 3, norm, z))
    one = jnp.ones_like(z)
    features = jnp.concatenate([high, high, mid, mid, high, low, one, jnp.zeros_like(z)], axis=0)
    weighted = share * jnp.where(quarter == 3, 1.0, z)
    first, second, _ = cut(weighted)
    return features.T.astype(BF16), jnp.concatenate([first, second], axis=0).astype(BF16)


def target_features(z):
    quarter = rows_of(z.shape[1]) & 3
    square = 0.5 * z * z
    norm = pltpu.roll(square, 1, 0) + pltpu.roll(square, 2, 0) + pltpu.roll(square, 3, 0)
    high, mid, low = cut(jnp.where(quarter == 3, norm, z))
    flat = quarter == 3
    own = jnp.where(
        flat,
        -high,
        jnp.where(quarter == 2, -pltpu.roll(mid, 7, 0), jnp.where(quarter == 1, -pltpu.roll(low, 6, 0), 0.0)),
    )
    high = jnp.where(flat, -1.0, high)
    mid = jnp.where(flat, 0.0, mid)
    low = jnp.where(flat, 0.0, low)
    return [high, mid, high, mid, low, high, own, jnp.zeros_like(z)]


def masked(groups, half):
    keep = (rows_of(groups[0].shape[1]) >> 2) == half
    return jnp.concatenate([jnp.where(keep, g, 0.0) for g in groups], axis=0).astype(BF16)


def weighted_sum(weighted, weight, pieces, flip):
    dims = (((1,), (1 if flip else 0,)), ((), ()))
    high = weight.astype(BF16)
    total = lax.dot_general(weighted, high, dims, preferred_element_type=F32)
    if pieces == 2:
        rest = (weight - high.astype(F32)).astype(BF16)
        total = total + lax.dot_general(weighted, rest, dims, preferred_element_type=F32)
    return total[:8] + total[8:]


def block_items(sources, weighted, targets, t, kind, others=None):
    items = []
    for h in range(2):
        rows = slice(h * HALF, (h + 1) * HALF)
        width = HALF if kind == "self" and h == 0 else PA
        flips = None
        if kind == "self" and h == 1:
            flips = (weighted, HALF, (t, 1))
        if kind == "cross":
            flips = (others, PA, (1, h))
        items.append((sources, rows, weighted, targets, width, t, flips))
    return items


def run_items(items, pieces, sums):
    waiting = None
    for item in list(items) + [None]:
        exponent = None
        if item is not None:
            sources, rows, _, targets, width = item[:5]
            exponent = jnp.dot(sources[rows, :], targets[:, :width], preferred_element_type=F32)
        if waiting is not None:
            (_, rows, weighted, _, width, t, flips), held = waiting
            weight = jnp.exp2(held)
            direct = weighted_sum(weighted[:, rows], weight, pieces, False)
            for half in range(width // HALF):
                part = direct[:, half * HALF:(half + 1) * HALF]
                sums[t, half] = sums[t, half] + part if (t, half) in sums else part
            if flips is not None:
                shares, depth, key = flips
                part = weighted_sum(shares[:, :depth], weight[:, :depth], pieces, True)
                sums[key] = sums[key] + part if key in sums else part
        waiting = (item, exponent)


def forces_of(z, sums):
    quarter = rows_of(z.shape[1]) & 3
    plain = jnp.where(quarter == 3, sums, 0.0)
    spread = pltpu.roll(plain, 7, 0) + pltpu.roll(plain, 6, 0) + pltpu.roll(plain, 5, 0)
    return jnp.where(quarter == 3, 0.0, z * spread - sums)


def kernel(
    nb, ns, planes_total,
    table, pos, vel, mass, amp, chg,
    moved, final,
    X, V, AF, AS, prm, prm_l, prm_r, halo_l, halo_r, ring_p, ring_n,
    part_s, part_r, Y, y_l, y_r, far_s, far_r,
    nST, nXS, nT, nG, fST, fXS, fT, fG,
    prm_ss, prm_rs, halo_ss, halo_rs, ring_ss, ring_rs, part_ss, part_rs, y_ss, y_rs, far_ss, far_rs,
):
    me_b = lax.axis_index("bead")
    me_s = lax.axis_index("slab")
    left = (me_b, lax.rem(me_s + ns - 1, ns))
    right = (me_b, lax.rem(me_s + 1, ns))
    prev = (lax.rem(me_b + nb - 1, nb), me_s)
    after = (lax.rem(me_b + 1, nb), me_s)
    pairs = X.shape[1]
    beads_here = 2 * pairs
    atoms = X.shape[3]
    first_bead = me_b * beads_here

    def remote(src, dst, ss, rs, to):
        return pltpu.make_async_remote_copy(
            src_ref=src, dst_ref=dst, send_sem=ss, recv_sem=rs, device_id=to, device_id_type=MESH
        )

    barrier = pltpu.get_barrier_semaphore()
    pl.semaphore_signal(barrier, inc=1, device_id=left, device_id_type=MESH)
    pl.semaphore_signal(barrier, inc=1, device_id=right, device_id_type=MESH)
    for d in range(1, nb):
        other = (lax.rem(me_b + d, nb), me_s)
        pl.semaphore_signal(barrier, inc=1, device_id=other, device_id_type=MESH)

    X[0] = jnp.zeros((pairs, 8, atoms), F32)
    V[...] = jnp.zeros_like(V)
    for b in range(beads_here):
        p, r = b // 2, 4 * (b % 2)
        for c in range(3):
            X[0, p, r + c:r + c + 1, :] = pos[c, b:b + 1, :]
            V[p, r + c:r + c + 1, :] = vel[c, b:b + 1, :]
    prm[...] = jnp.zeros_like(prm)
    for t in range(2):
        lanes = slice(t * PA, (t + 1) * PA)
        prm[t:t + 1, :] = amp[:, lanes]
        prm[2 + t:3 + t, :] = chg[:, lanes]

    pl.semaphore_wait(barrier, nb + 1)

    prm_copies = [
        remote(prm, prm_r, prm_ss.at[0], prm_rs.at[0], left),
        remote(prm, prm_l, prm_ss.at[1], prm_rs.at[1], right),
    ]
    for copy in prm_copies:
        copy.start()

    centre = (me_s * 2).astype(F32) + 1.0
    span = float(planes_total)
    centre_l = centre + jnp.where(me_s == 0, span, 0.0)
    centre_r = centre - jnp.where(me_s == ns - 1, span, 0.0)
    near_rate = math.sqrt(near_scale / math.log(2.0))
    far_rate = math.sqrt(far_scale / math.log(2.0))

    inverse = 1.0 / mass[...]

    def halo_copies(k):
        return [
            remote(X.at[k, :, :, pl.ds(0, PA)], halo_r.at[k], halo_ss.at[k, 0], halo_rs.at[k, 0], left),
            remote(X.at[k, :, :, pl.ds(atoms - PA, PA)], halo_l.at[k], halo_ss.at[k, 1], halo_rs.at[k, 1], right),
        ]

    def ring_copies(k):
        return [
            remote(X.at[k, pairs - 1], ring_p.at[k], ring_ss.at[k, 0], ring_rs.at[k, 0], after),
            remote(X.at[k, 0], ring_n.at[k], ring_ss.at[k, 1], ring_rs.at[k, 1], prev),
        ]

    def spoke_copies(src, dst, ss, rs, e):
        return [
            remote(src(d), dst.at[e, d], ss.at[e, d], rs.at[e, d], (lax.rem(me_b + d, nb), me_s))
            for d in range(1, nb)
        ]

    def part_copies(e):
        return spoke_copies(lambda d: part_s.at[e, d], part_r, part_ss, part_rs, e)

    def far_copies(e):
        return spoke_copies(lambda d: far_s.at[e], far_r, far_ss, far_rs, e)

    def y_copies(e):
        return [
            remote(Y.at[e], y_r.at[e], y_ss.at[e, 0], y_rs.at[e, 0], left),
            remote(Y.at[e], y_l.at[e], y_ss.at[e, 1], y_rs.at[e, 1], right),
        ]

    low_rows = rows_of(PA) < 4

    def partial_of(k, c):
        total = None
        for p in range(pairs):
            first = table[c, first_bead + 2 * p]
            second = table[c, first_bead + 2 * p + 1]
            term = jnp.where(rows_of(atoms) < 4, first, second) * X[k, p]
            total = term if total is None else total + term
        total = total + pltpu.roll(total, 4, 0)
        return jnp.where(low_rows, total[:, :PA], total[:, PA:])

    def far_halves(tile):
        first = jnp.where(low_rows, tile, 0.0)
        second = jnp.where(low_rows, pltpu.roll(tile, 4, 0), 0.0)
        return first, second

    def near_items(p, part, blocks):
        items = []
        for t, q, kind in blocks:
            others = nXS.at[p, 1] if kind == "cross" else None
            items += block_items(nST.at[p, q], nXS.at[p, q], nT.at[p, t, part], t, kind, others)
        return items

    def near_blocks(p, blocks, first):
        sums = ({}, {})
        for part in range(2):
            run_items(near_items(p, part, blocks), 1, sums[part])
        for t, half in sums[0]:
            lanes = slice(half * HALF, (half + 1) * HALF)
            both = jnp.where(rows_of(HALF) < 4, sums[0][t, half], sums[1][t, half])
            if first:
                nG[p, t, :, lanes] = both
            else:
                nG[p, t, :, lanes] += both

    def far_blocks(blocks, first):
        items, sums = [], {}
        for t, q, kind in blocks:
            others = fXS.at[2] if kind == "cross" else None
            items += block_items(fST.at[q], fXS.at[q], fT.at[t], t, kind, others)
        run_items(items, 2, sums)
        for t, half in sums:
            lanes = slice(half * HALF, (half + 1) * HALF)
            if first:
                fG[t, :, lanes] = sums[t, half]
            else:
                fG[t, :, lanes] += sums[t, half]

    near_own = ((0, 1, "self"), (0, 2, "cross"), (1, 2, "self"))
    near_rim = ((0, 0, "rim"), (1, 3, "rim"))
    far_own = ((0, 2, "self"), (0, 3, "cross"), (1, 3, "self"))
    far_rim = ((0, 0, "rim"), (0, 1, "rim"), (0, 4, "rim"), (1, 1, "rim"), (1, 4, "rim"), (1, 5, "rim"))

    def phase(k, carry):
        slow_turn = lax.rem(k, INNER_STEPS) == 0
        e = k // INNER_STEPS
        for copy in halo_copies(k):
            copy.start()

        @pl.when(slow_turn)
        def _():
            for d in range(1, nb):
                part_s[e, d] = partial_of(k, lax.rem(me_b + d, nb))
            for copy in part_copies(e):
                copy.start()

        for copy in ring_copies(k):
            copy.start()

        for p in range(pairs):
            for t in range(2):
                lanes = slice(t * PA, (t + 1) * PA)
                z = scaled(X[k, p, :, lanes], centre, near_rate)
                nST[p, 1 + t], nXS[p, 1 + t] = source_features(z, amp[:, lanes])
                groups = target_features(z)
                nT[p, t, 0] = masked(groups, 0)
                nT[p, t, 1] = masked(groups, 1)

        @pl.when(k == 0)
        def _():
            for copy in prm_copies:
                copy.wait_recv()

        @pl.loop(0, pairs // 2)
        def _(p):
            near_blocks(p, near_own, True)

        @pl.when(slow_turn)
        def _():
            total = partial_of(k, me_b)
            for d, copy in enumerate(part_copies(e)):
                copy.wait_recv()
                total = total + part_r[e, d + 1]
            Y[e] = total
            for copy in y_copies(e):
                copy.start()

        @pl.loop(pairs // 2, pairs)
        def _(p):
            near_blocks(p, near_own, True)

        @pl.when(slow_turn)
        def _():
            for t, half in enumerate(far_halves(Y[e])):
                z = scaled(half, centre, far_rate)
                z = jnp.where(low_rows, z, 0.0)
                fST[2 + t], fXS[2 + t] = source_features(z, chg[:, t * PA:(t + 1) * PA])
                fT[t] = masked(target_features(z), 0)
            far_blocks(far_own, True)

        for copy in halo_copies(k):
            copy.wait_recv()
        for p in range(pairs):
            z = scaled(halo_l[k, p], centre_l, near_rate)
            nST[p, 0], nXS[p, 0] = source_features(z, prm_l[1:2, :])
            z = scaled(halo_r[k, p], centre_r, near_rate)
            nST[p, 3], nXS[p, 3] = source_features(z, prm_r[0:1, :])

        @pl.loop(0, pairs)
        def _(p):
            near_blocks(p, near_rim, False)

        @pl.when(slow_turn)
        def _():
            for copy in y_copies(e):
                copy.wait_recv()
            for base, tile, shares, middle in ((0, y_l, prm_l, centre_l), (4, y_r, prm_r, centre_r)):
                for t, half in enumerate(far_halves(tile[e])):
                    z = scaled(half, middle, far_rate)
                    z = jnp.where(low_rows, z, 0.0)
                    fST[base + t], fXS[base + t] = source_features(z, shares[2 + t:3 + t, :])
            far_blocks(far_rim, False)
            halves = []
            for t, half in enumerate(far_halves(Y[e])):
                lanes = slice(t * PA, (t + 1) * PA)
                z = scaled(half, centre, far_rate)
                coefficient = chg[:, lanes] * (far_scale / far_rate)
                halves.append(coefficient * forces_of(z, fG[t]))
            far_s[e] = jnp.where(low_rows, halves[0], pltpu.roll(halves[1], 4, 0))
            for copy in far_copies(e):
                copy.start()

        for copy in ring_copies(k):
            copy.wait_recv()
        upper = rows_of(atoms) < 4
        rolled = [pltpu.roll(X[k, p], 4, 0) for p in range(pairs)]
        before = [pltpu.roll(ring_p[k], 4, 0)] + rolled
        behind = rolled + [pltpu.roll(ring_n[k], 4, 0)]
        for p in range(pairs):
            springs = 2.0 * X[k, p] - rolled[p] - jnp.where(upper, before[p], behind[p + 1])
            AF[p] = -spring_rate * springs
            for t in range(2):
                lanes = slice(t * PA, (t + 1) * PA)
                z = scaled(X[k, p, :, lanes], centre, near_rate)
                coefficient = amp[:, lanes] * (near_scale / near_rate) * inverse[:, lanes]
                AF[p, :, lanes] += coefficient * forces_of(z, nG[p, t])

        edge = (k == 0) | (k == PHASES - 1)
        fast_step = jnp.where(edge, 0.5 * time_step, time_step)
        slow_step = jnp.where(edge, 0.5 * INNER_STEPS * time_step, INNER_STEPS * time_step)
        for p in range(pairs):
            V[p] += fast_step * AF[p]

        @pl.when(slow_turn)
        def _():
            for copy in far_copies(e):
                copy.wait_recv()
            ratio = float(beads_here)
            total = [[None, None] for _ in range(pairs)]
            for d in range(nb):
                tile = far_s[e] if d == 0 else far_r[e, d]
                c = lax.rem(me_b + nb - d, nb)
                turned = pltpu.roll(tile, 4, 0)
                doubled = (jnp.where(low_rows, tile, turned), jnp.where(low_rows, turned, tile))
                for p in range(pairs):
                    first = table[c, first_bead + 2 * p] * ratio
                    second = table[c, first_bead + 2 * p + 1] * ratio
                    level = jnp.where(low_rows, first, second)
                    for t in range(2):
                        term = level * doubled[t]
                        total[p][t] = term if d == 0 else total[p][t] + term
            for p in range(pairs):
                for t in range(2):
                    lanes = slice(t * PA, (t + 1) * PA)
                    V[p, :, lanes] += slow_step * inverse[:, lanes] * total[p][t]

        @pl.when(k < PHASES - 1)
        def _():
            for p in range(pairs):
                X[k + 1, p] = X[k, p] + time_step * V[p]

        return carry

    lax.fori_loop(0, PHASES, phase, 0)

    last = PHASES - 1
    for b in range(beads_here):
        p, r = b // 2, 4 * (b % 2)
        for c in range(3):
            moved[c, b:b + 1, :] = X[last, p, r + c:r + c + 1, :] - pos[c, b:b + 1, :]
            final[c, b:b + 1, :] = V[p, r + c:r + c + 1, :]

    for copy in prm_copies:
        copy.wait_send()

    @pl.loop(0, PHASES)
    def _(k):
        for copy in halo_copies(k) + ring_copies(k):
            copy.wait_send()

    @pl.loop(0, EVENTS)
    def _(e):
        for copy in part_copies(e) + y_copies(e) + far_copies(e):
            copy.wait_send()


def solution(mesh):
    nb, ns = mesh.shape["bead"], mesh.shape["slab"]

    def shards(positions, velocities, masses, amplitudes, charges):
        beads_here, _, atoms = positions.shape
        assert atoms == 2 * PA and beads_here % 2 == 0
        pairs = beads_here // 2
        table = jnp.asarray(contraction(beads_here * nb, nb))
        vmem = pl.BlockSpec(memory_space=pltpu.VMEM)
        out = jax.ShapeDtypeStruct((3, beads_here, atoms), F32)
        V, D = pltpu.VMEM, pltpu.SemaphoreType.DMA
        tile = (8, PA)

        def body(*refs):
            kernel(nb, ns, 2 * ns, *refs)

        shifted, speeds = pl.pallas_call(
            body,
            name="rod",
            out_shape=(out, out),
            in_specs=[pl.BlockSpec(memory_space=pltpu.SMEM)] + [vmem] * 5,
            out_specs=(vmem, vmem),
            scratch_shapes=[
                V((PHASES, pairs, 8, atoms), F32),
                V((pairs, 8, atoms), F32),
                V((pairs, 8, atoms), F32),
                V((pairs, 8, atoms), F32),
                V(tile, F32), V(tile, F32), V(tile, F32),
                V((PHASES, pairs) + tile, F32), V((PHASES, pairs) + tile, F32),
                V((PHASES, 8, atoms), F32), V((PHASES, 8, atoms), F32),
                V((EVENTS, nb) + tile, F32), V((EVENTS, nb) + tile, F32),
                V((EVENTS,) + tile, F32), V((EVENTS,) + tile, F32), V((EVENTS,) + tile, F32),
                V((EVENTS,) + tile, F32), V((EVENTS, nb) + tile, F32),
                V((pairs, 4, PA, FEATURES), BF16), V((pairs, 4, 16, PA), BF16),
                V((pairs, 2, 2, FEATURES, PA), BF16), V((pairs, 2) + tile, F32),
                V((6, PA, FEATURES), BF16), V((6, 16, PA), BF16),
                V((2, FEATURES, PA), BF16), V((2,) + tile, F32),
                D((2,)), D((2,)), D((PHASES, 2)), D((PHASES, 2)), D((PHASES, 2)), D((PHASES, 2)),
                D((EVENTS, nb)), D((EVENTS, nb)), D((EVENTS, 2)), D((EVENTS, 2)),
                D((EVENTS, nb)), D((EVENTS, nb)),
            ],
            compiler_params=pltpu.CompilerParams(collective_id=0, has_side_effects=True),
        )(table, positions.transpose(1, 0, 2), velocities.transpose(1, 0, 2), masses[None], amplitudes[None], charges[None])
        return shifted.transpose(1, 0, 2), speeds.transpose(1, 0, 2)

    both = P("bead", None, "slab")
    return jax.shard_map(
        shards, mesh=mesh, in_specs=(both, both, P("slab"), P("slab"), P("slab")), out_specs=(both, both), check_vma=False
    )
```

```python
import math

import jax
import jax.numpy as jnp
import numpy as np
from jax import lax
from jax.experimental import pallas as pl
from jax.experimental.pallas import tpu as pltpu
from jax.sharding import PartitionSpec as P

INNER_STEPS = 2
OUTER_STEPS = 2
PLANE_ATOMS = 512

time_step = 0.05
spring_rate = 25.0
near_scale = 4.0
far_scale = 2.0

MESH = pl.DeviceIdType.MESH
F32 = jnp.float32
BF16 = jnp.bfloat16
PA = PLANE_ATOMS
PHASES = INNER_STEPS * OUTER_STEPS + 1
EVENTS = OUTER_STEPS + 1
FEATURES = 64
HALF = PA // 2


def contraction(bead_count, small_count):
    bead_place = np.arange(bead_count, dtype=np.float64) / bead_count
    small_place = np.arange(small_count, dtype=np.float64) / small_count
    phase = 2.0 * np.pi * (bead_place[None, :] - small_place[:, None])
    modes = np.arange(1, small_count // 2, dtype=np.float64)
    total = 1.0 + np.cos(0.5 * small_count * phase)
    total = total + 2.0 * np.sum(np.cos(modes[:, None, None] * phase[None]), axis=0)
    return (total / bead_count).astype(np.float32)


def rows_of(width):
    return lax.broadcasted_iota(jnp.int32, (8, width), 0)


def cut(x):
    high = x.astype(BF16).astype(F32)
    rest = x - high
    mid = rest.astype(BF16).astype(F32)
    low = (rest - mid).astype(BF16).astype(F32)
    return high, mid, low


def scaled(x, first_centre, rate):
    quarter = rows_of(x.shape[1]) & 3
    centre = jnp.where(quarter == 0, first_centre, jnp.where(quarter == 3, 0.0, 1.0))
    return (x - centre) * rate


def source_features(z, share):
    quarter = rows_of(z.shape[1]) & 3
    square = 0.5 * z * z
    norm = pltpu.roll(square, 1, 0) + pltpu.roll(square, 2, 0) + pltpu.roll(square, 3, 0)
    high, mid, low = cut(jnp.where(quarter == 3, norm, z))
    one = jnp.ones_like(z)
    features = jnp.concatenate([high, high, mid, mid, high, low, one, jnp.zeros_like(z)], axis=0)
    weighted = share * jnp.where(quarter == 3, 1.0, z)
    first, second, _ = cut(weighted)
    return features.T.astype(BF16), jnp.concatenate([first, second], axis=0).astype(BF16)


def target_features(z):
    quarter = rows_of(z.shape[1]) & 3
    square = 0.5 * z * z
    norm = pltpu.roll(square, 1, 0) + pltpu.roll(square, 2, 0) + pltpu.roll(square, 3, 0)
    high, mid, low = cut(jnp.where(quarter == 3, norm, z))
    flat = quarter == 3
    own = jnp.where(
        flat,
        -high,
        jnp.where(quarter == 2, -pltpu.roll(mid, 7, 0), jnp.where(quarter == 1, -pltpu.roll(low, 6, 0), 0.0)),
    )
    high = jnp.where(flat, -1.0, high)
    mid = jnp.where(flat, 0.0, mid)
    low = jnp.where(flat, 0.0, low)
    return [high, mid, high, mid, low, high, own, jnp.zeros_like(z)]


def masked(groups, half):
    keep = (rows_of(groups[0].shape[1]) >> 2) == half
    return jnp.concatenate([jnp.where(keep, g, 0.0) for g in groups], axis=0).astype(BF16)


def weighted_sum(weighted, weight, pieces, flip):
    dims = (((1,), (1 if flip else 0,)), ((), ()))
    high = weight.astype(BF16)
    total = lax.dot_general(weighted, high, dims, preferred_element_type=F32)
    if pieces == 2:
        rest = (weight - high.astype(F32)).astype(BF16)
        total = total + lax.dot_general(weighted, rest, dims, preferred_element_type=F32)
    return total[:8] + total[8:]


def block_items(sources, weighted, targets, t, kind, others=None):
    items = []
    for h in range(2):
        rows = slice(h * HALF, (h + 1) * HALF)
        width = HALF if kind == "self" and h == 0 else PA
        flips = None
        if kind == "self" and h == 1:
            flips = (weighted, HALF, (t, 1))
        if kind == "cross":
            flips = (others, PA, (1, h))
        items.append((sources, rows, weighted, targets, width, t, flips))
    return items


def run_items(items, pieces):
    waiting = None
    for item, sums_of in list(items) + [(None, None)]:
        exponent = None
        if item is not None:
            sources, rows, _, targets, width = item[:5]
            exponent = jnp.dot(sources[rows, :], targets[:, :width], preferred_element_type=F32)
        if waiting is not None:
            (_, rows, weighted, _, width, t, flips), held, sums = waiting
            weight = jnp.exp2(held)
            direct = weighted_sum(weighted[:, rows], weight, pieces, False)
            for half in range(width // HALF):
                part = direct[:, half * HALF:(half + 1) * HALF]
                sums[t, half] = sums[t, half] + part if (t, half) in sums else part
            if flips is not None:
                shares, depth, key = flips
                part = weighted_sum(shares[:, :depth], weight[:, :depth], pieces, True)
                sums[key] = sums[key] + part if key in sums else part
        waiting = (item, exponent, sums_of)


def forces_of(z, sums):
    quarter = rows_of(z.shape[1]) & 3
    plain = jnp.where(quarter == 3, sums, 0.0)
    spread = pltpu.roll(plain, 7, 0) + pltpu.roll(plain, 6, 0) + pltpu.roll(plain, 5, 0)
    return jnp.where(quarter == 3, 0.0, z * spread - sums)


def kernel(
    nb, ns, planes_total,
    table, pos, vel, mass, amp, chg,
    moved, final,
    X, V, AF, AS, prm, prm_l, prm_r, halo_l, halo_r, ring_p, ring_n,
    part_s, part_r, Y, y_l, y_r, far_s, far_r,
    nST, nXS, nT, nG, fST, fXS, fT, fG,
    prm_ss, prm_rs, halo_ss, halo_rs, ring_ss, ring_rs, part_ss, part_rs, y_ss, y_rs, far_ss, far_rs,
):
    me_b = lax.axis_index("bead")
    me_s = lax.axis_index("slab")
    left = (me_b, lax.rem(me_s + ns - 1, ns))
    right = (me_b, lax.rem(me_s + 1, ns))
    prev = (lax.rem(me_b + nb - 1, nb), me_s)
    after = (lax.rem(me_b + 1, nb), me_s)
    pairs = X.shape[1]
    beads_here = 2 * pairs
    atoms = X.shape[3]
    first_bead = me_b * beads_here

    def remote(src, dst, ss, rs, to):
        return pltpu.make_async_remote_copy(
            src_ref=src, dst_ref=dst, send_sem=ss, recv_sem=rs, device_id=to, device_id_type=MESH
        )

    barrier = pltpu.get_barrier_semaphore()
    pl.semaphore_signal(barrier, inc=1, device_id=left, device_id_type=MESH)
    pl.semaphore_signal(barrier, inc=1, device_id=right, device_id_type=MESH)
    for d in range(1, nb):
        other = (lax.rem(me_b + d, nb), me_s)
        pl.semaphore_signal(barrier, inc=1, device_id=other, device_id_type=MESH)

    X[0] = jnp.zeros((pairs, 8, atoms), F32)
    V[...] = jnp.zeros_like(V)
    for b in range(beads_here):
        p, r = b // 2, 4 * (b % 2)
        for c in range(3):
            X[0, p, r + c:r + c + 1, :] = pos[c, b:b + 1, :]
            V[p, r + c:r + c + 1, :] = vel[c, b:b + 1, :]
    prm[...] = jnp.zeros_like(prm)
    for t in range(2):
        lanes = slice(t * PA, (t + 1) * PA)
        prm[t:t + 1, :] = amp[:, lanes]
        prm[2 + t:3 + t, :] = chg[:, lanes]

    pl.semaphore_wait(barrier, nb + 1)

    prm_copies = [
        remote(prm, prm_r, prm_ss.at[0], prm_rs.at[0], left),
        remote(prm, prm_l, prm_ss.at[1], prm_rs.at[1], right),
    ]
    for copy in prm_copies:
        copy.start()

    centre = (me_s * 2).astype(F32) + 1.0
    span = float(planes_total)
    centre_l = centre + jnp.where(me_s == 0, span, 0.0)
    centre_r = centre - jnp.where(me_s == ns - 1, span, 0.0)
    near_rate = math.sqrt(near_scale / math.log(2.0))
    far_rate = math.sqrt(far_scale / math.log(2.0))

    inverse = 1.0 / mass[...]

    def halo_copies(k):
        return [
            remote(X.at[k, :, :, pl.ds(0, PA)], halo_r.at[k], halo_ss.at[k, 0], halo_rs.at[k, 0], left),
            remote(X.at[k, :, :, pl.ds(atoms - PA, PA)], halo_l.at[k], halo_ss.at[k, 1], halo_rs.at[k, 1], right),
        ]

    def ring_copies(k):
        return [
            remote(X.at[k, pairs - 1], ring_p.at[k], ring_ss.at[k, 0], ring_rs.at[k, 0], after),
            remote(X.at[k, 0], ring_n.at[k], ring_ss.at[k, 1], ring_rs.at[k, 1], prev),
        ]

    def spoke_copies(src, dst, ss, rs, e):
        return [
            remote(src(d), dst.at[e, d], ss.at[e, d], rs.at[e, d], (lax.rem(me_b + d, nb), me_s))
            for d in range(1, nb)
        ]

    def part_copies(e):
        return spoke_copies(lambda d: part_s.at[e, d], part_r, part_ss, part_rs, e)

    def far_copies(e):
        return spoke_copies(lambda d: far_s.at[e], far_r, far_ss, far_rs, e)

    def y_copies(e):
        return [
            remote(Y.at[e], y_r.at[e], y_ss.at[e, 0], y_rs.at[e, 0], left),
            remote(Y.at[e], y_l.at[e], y_ss.at[e, 1], y_rs.at[e, 1], right),
        ]

    low_rows = rows_of(PA) < 4

    def partial_of(k, c):
        total = None
        for p in range(pairs):
            first = table[c, first_bead + 2 * p]
            second = table[c, first_bead + 2 * p + 1]
            term = jnp.where(rows_of(atoms) < 4, first, second) * X[k, p]
            total = term if total is None else total + term
        total = total + pltpu.roll(total, 4, 0)
        return jnp.where(low_rows, total[:, :PA], total[:, PA:])

    def far_halves(tile):
        first = jnp.where(low_rows, tile, 0.0)
        second = jnp.where(low_rows, pltpu.roll(tile, 4, 0), 0.0)
        return first, second

    def near_items(p, part, blocks):
        items = []
        for t, q, kind in blocks:
            others = nXS.at[p, 1] if kind == "cross" else None
            items += block_items(nST.at[p, q], nXS.at[p, q], nT.at[p, t, part], t, kind, others)
        return items

    def near_blocks(p, blocks, first):
        sums = ({}, {})
        run_items([(item, sums[part]) for part in range(2) for item in near_items(p, part, blocks)], 1)
        for t, half in sums[0]:
            lanes = slice(half * HALF, (half + 1) * HALF)
            both = jnp.where(rows_of(HALF) < 4, sums[0][t, half], sums[1][t, half])
            if first:
                nG[p, t, :, lanes] = both
            else:
                nG[p, t, :, lanes] += both

    def far_blocks(blocks, first):
        items, sums = [], {}
        for t, q, kind in blocks:
            others = fXS.at[2] if kind == "cross" else None
            items += block_items(fST.at[q], fXS.at[q], fT.at[t], t, kind, others)
        run_items([(item, sums) for item in items], 2)
        for t, half in sums:
            lanes = slice(half * HALF, (half + 1) * HALF)
            if first:
                fG[t, :, lanes] = sums[t, half]
            else:
                fG[t, :, lanes] += sums[t, half]

    near_own = ((0, 1, "self"), (0, 2, "cross"), (1, 2, "self"))
    near_rim = ((0, 0, "rim"), (1, 3, "rim"))
    far_own = ((0, 2, "self"), (0, 3, "cross"), (1, 3, "self"))
    far_rim = ((0, 0, "rim"), (0, 1, "rim"), (0, 4, "rim"), (1, 1, "rim"), (1, 4, "rim"), (1, 5, "rim"))

    def phase(k, carry):
        slow_turn = lax.rem(k, INNER_STEPS) == 0
        e = k // INNER_STEPS
        for copy in halo_copies(k):
            copy.start()

        @pl.when(slow_turn)
        def _():
            for d in range(1, nb):
                part_s[e, d] = partial_of(k, lax.rem(me_b + d, nb))
            for copy in part_copies(e):
                copy.start()

        for copy in ring_copies(k):
            copy.start()

        for p in range(pairs):
            for t in range(2):
                lanes = slice(t * PA, (t + 1) * PA)
                z = scaled(X[k, p, :, lanes], centre, near_rate)
                nST[p, 1 + t], nXS[p, 1 + t] = source_features(z, amp[:, lanes])
                groups = target_features(z)
                nT[p, t, 0] = masked(groups, 0)
                nT[p, t, 1] = masked(groups, 1)

        @pl.when(k == 0)
        def _():
            for copy in prm_copies:
                copy.wait_recv()

        @pl.loop(0, pairs // 2)
        def _(p):
            near_blocks(p, near_own, True)

        @pl.when(slow_turn)
        def _():
            total = partial_of(k, me_b)
            for d, copy in enumerate(part_copies(e)):
                copy.wait_recv()
                total = total + part_r[e, d + 1]
            Y[e] = total
            for copy in y_copies(e):
                copy.start()

        @pl.loop(pairs // 2, pairs)
        def _(p):
            near_blocks(p, near_own, True)

        @pl.when(slow_turn)
        def _():
            for t, half in enumerate(far_halves(Y[e])):
                z = scaled(half, centre, far_rate)
                z = jnp.where(low_rows, z, 0.0)
                fST[2 + t], fXS[2 + t] = source_features(z, chg[:, t * PA:(t + 1) * PA])
                fT[t] = masked(target_features(z), 0)
            far_blocks(far_own, True)

        for copy in halo_copies(k):
            copy.wait_recv()
        for p in range(pairs):
            z = scaled(halo_l[k, p], centre_l, near_rate)
            nST[p, 0], nXS[p, 0] = source_features(z, prm_l[1:2, :])
            z = scaled(halo_r[k, p], centre_r, near_rate)
            nST[p, 3], nXS[p, 3] = source_features(z, prm_r[0:1, :])

        @pl.loop(0, pairs // 2)
        def _(p):
            near_blocks(p, near_rim, False)

        @pl.when(slow_turn)
        def _():
            for copy in y_copies(e):
                copy.wait_recv()
            for base, tile, shares, middle in ((0, y_l, prm_l, centre_l), (4, y_r, prm_r, centre_r)):
                for t, half in enumerate(far_halves(tile[e])):
                    z = scaled(half, middle, far_rate)
                    z = jnp.where(low_rows, z, 0.0)
                    fST[base + t], fXS[base + t] = source_features(z, shares[2 + t:3 + t, :])
            far_blocks(far_rim, False)
            halves = []
            for t, half in enumerate(far_halves(Y[e])):
                lanes = slice(t * PA, (t + 1) * PA)
                z = scaled(half, centre, far_rate)
                coefficient = chg[:, lanes] * (far_scale / far_rate)
                halves.append(coefficient * forces_of(z, fG[t]))
            far_s[e] = jnp.where(low_rows, halves[0], pltpu.roll(halves[1], 4, 0))
            for copy in far_copies(e):
                copy.start()

        @pl.loop(pairs // 2, pairs)
        def _(p):
            near_blocks(p, near_rim, False)

        for copy in ring_copies(k):
            copy.wait_recv()
        upper = rows_of(atoms) < 4
        rolled = [pltpu.roll(X[k, p], 4, 0) for p in range(pairs)]
        before = [pltpu.roll(ring_p[k], 4, 0)] + rolled
        behind = rolled + [pltpu.roll(ring_n[k], 4, 0)]
        for p in range(pairs):
            springs = 2.0 * X[k, p] - rolled[p] - jnp.where(upper, before[p], behind[p + 1])
            AF[p] = -spring_rate * springs
            for t in range(2):
                lanes = slice(t * PA, (t + 1) * PA)
                z = scaled(X[k, p, :, lanes], centre, near_rate)
                coefficient = amp[:, lanes] * (near_scale / near_rate) * inverse[:, lanes]
                AF[p, :, lanes] += coefficient * forces_of(z, nG[p, t])

        edge = (k == 0) | (k == PHASES - 1)
        fast_step = jnp.where(edge, 0.5 * time_step, time_step)
        slow_step = jnp.where(edge, 0.5 * INNER_STEPS * time_step, INNER_STEPS * time_step)
        for p in range(pairs):
            V[p] += fast_step * AF[p]

        @pl.when(slow_turn)
        def _():
            for copy in far_copies(e):
                copy.wait_recv()
            ratio = float(beads_here)
            total = [[None, None] for _ in range(pairs)]
            for d in range(nb):
                tile = far_s[e] if d == 0 else far_r[e, d]
                c = lax.rem(me_b + nb - d, nb)
                turned = pltpu.roll(tile, 4, 0)
                doubled = (jnp.where(low_rows, tile, turned), jnp.where(low_rows, turned, tile))
                for p in range(pairs):
                    first = table[c, first_bead + 2 * p] * ratio
                    second = table[c, first_bead + 2 * p + 1] * ratio
                    level = jnp.where(low_rows, first, second)
                    for t in range(2):
                        term = level * doubled[t]
                        total[p][t] = term if d == 0 else total[p][t] + term
            for p in range(pairs):
                for t in range(2):
                    lanes = slice(t * PA, (t + 1) * PA)
                    V[p, :, lanes] += slow_step * inverse[:, lanes] * total[p][t]

        @pl.when(k < PHASES - 1)
        def _():
            for p in range(pairs):
                X[k + 1, p] = X[k, p] + time_step * V[p]

        return carry

    lax.fori_loop(0, PHASES, phase, 0)

    last = PHASES - 1
    for b in range(beads_here):
        p, r = b // 2, 4 * (b % 2)
        for c in range(3):
            moved[c, b:b + 1, :] = X[last, p, r + c:r + c + 1, :] - pos[c, b:b + 1, :]
            final[c, b:b + 1, :] = V[p, r + c:r + c + 1, :]

    for copy in prm_copies:
        copy.wait_send()

    @pl.loop(0, PHASES)
    def _(k):
        for copy in halo_copies(k) + ring_copies(k):
            copy.wait_send()

    @pl.loop(0, EVENTS)
    def _(e):
        for copy in part_copies(e) + y_copies(e) + far_copies(e):
            copy.wait_send()


def solution(mesh):
    nb, ns = mesh.shape["bead"], mesh.shape["slab"]

    def shards(positions, velocities, masses, amplitudes, charges):
        beads_here, _, atoms = positions.shape
        assert atoms == 2 * PA and beads_here % 2 == 0
        pairs = beads_here // 2
        table = jnp.asarray(contraction(beads_here * nb, nb))
        vmem = pl.BlockSpec(memory_space=pltpu.VMEM)
        out = jax.ShapeDtypeStruct((3, beads_here, atoms), F32)
        V, D = pltpu.VMEM, pltpu.SemaphoreType.DMA
        tile = (8, PA)

        def body(*refs):
            kernel(nb, ns, 2 * ns, *refs)

        shifted, speeds = pl.pallas_call(
            body,
            name="rod",
            out_shape=(out, out),
            in_specs=[pl.BlockSpec(memory_space=pltpu.SMEM)] + [vmem] * 5,
            out_specs=(vmem, vmem),
            scratch_shapes=[
                V((PHASES, pairs, 8, atoms), F32),
                V((pairs, 8, atoms), F32),
                V((pairs, 8, atoms), F32),
                V((pairs, 8, atoms), F32),
                V(tile, F32), V(tile, F32), V(tile, F32),
                V((PHASES, pairs) + tile, F32), V((PHASES, pairs) + tile, F32),
                V((PHASES, 8, atoms), F32), V((PHASES, 8, atoms), F32),
                V((EVENTS, nb) + tile, F32), V((EVENTS, nb) + tile, F32),
                V((EVENTS,) + tile, F32), V((EVENTS,) + tile, F32), V((EVENTS,) + tile, F32),
                V((EVENTS,) + tile, F32), V((EVENTS, nb) + tile, F32),
                V((pairs, 4, PA, FEATURES), BF16), V((pairs, 4, 16, PA), BF16),
                V((pairs, 2, 2, FEATURES, PA), BF16), V((pairs, 2) + tile, F32),
                V((6, PA, FEATURES), BF16), V((6, 16, PA), BF16),
                V((2, FEATURES, PA), BF16), V((2,) + tile, F32),
                D((2,)), D((2,)), D((PHASES, 2)), D((PHASES, 2)), D((PHASES, 2)), D((PHASES, 2)),
                D((EVENTS, nb)), D((EVENTS, nb)), D((EVENTS, 2)), D((EVENTS, 2)),
                D((EVENTS, nb)), D((EVENTS, nb)),
            ],
            compiler_params=pltpu.CompilerParams(collective_id=0, has_side_effects=True),
        )(table, positions.transpose(1, 0, 2), velocities.transpose(1, 0, 2), masses[None], amplitudes[None], charges[None])
        return shifted.transpose(1, 0, 2), speeds.transpose(1, 0, 2)

    both = P("bead", None, "slab")
    return jax.shard_map(
        shards, mesh=mesh, in_specs=(both, both, P("slab"), P("slab"), P("slab")), out_specs=(both, both), check_vma=False
    )
```

```python
import math

import jax
import jax.numpy as jnp
import numpy as np
from jax import lax
from jax.experimental import pallas as pl
from jax.experimental.pallas import tpu as pltpu
from jax.sharding import PartitionSpec as P

INNER_STEPS = 2
OUTER_STEPS = 2
PLANE_ATOMS = 512

time_step = 0.05
spring_rate = 25.0
near_scale = 4.0
far_scale = 2.0

MESH = pl.DeviceIdType.MESH
F32 = jnp.float32
BF16 = jnp.bfloat16
PA = PLANE_ATOMS
PHASES = INNER_STEPS * OUTER_STEPS + 1
EVENTS = OUTER_STEPS + 1
FEATURES = 64
HALF = PA // 2


def contraction(bead_count, small_count):
    bead_place = np.arange(bead_count, dtype=np.float64) / bead_count
    small_place = np.arange(small_count, dtype=np.float64) / small_count
    phase = 2.0 * np.pi * (bead_place[None, :] - small_place[:, None])
    modes = np.arange(1, small_count // 2, dtype=np.float64)
    total = 1.0 + np.cos(0.5 * small_count * phase)
    total = total + 2.0 * np.sum(np.cos(modes[:, None, None] * phase[None]), axis=0)
    return (total / bead_count).astype(np.float32)


def rows_of(width):
    return lax.broadcasted_iota(jnp.int32, (8, width), 0)


def cut(x):
    high = x.astype(BF16).astype(F32)
    rest = x - high
    mid = rest.astype(BF16).astype(F32)
    low = (rest - mid).astype(BF16).astype(F32)
    return high, mid, low


def scaled(x, first_centre, rate):
    quarter = rows_of(x.shape[1]) & 3
    centre = jnp.where(quarter == 0, first_centre, jnp.where(quarter == 3, 0.0, 1.0))
    return (x - centre) * rate


def source_features(z, share):
    quarter = rows_of(z.shape[1]) & 3
    square = 0.5 * z * z
    norm = pltpu.roll(square, 1, 0) + pltpu.roll(square, 2, 0) + pltpu.roll(square, 3, 0)
    high, mid, low = cut(jnp.where(quarter == 3, norm, z))
    one = jnp.ones_like(z)
    features = jnp.concatenate([high, high, mid, mid, high, low, one, jnp.zeros_like(z)], axis=0)
    weighted = share * jnp.where(quarter == 3, 1.0, z)
    first, second, _ = cut(weighted)
    return features.T.astype(BF16), jnp.concatenate([first, second], axis=0).astype(BF16)


def target_features(z):
    quarter = rows_of(z.shape[1]) & 3
    square = 0.5 * z * z
    norm = pltpu.roll(square, 1, 0) + pltpu.roll(square, 2, 0) + pltpu.roll(square, 3, 0)
    high, mid, low = cut(jnp.where(quarter == 3, norm, z))
    flat = quarter == 3
    own = jnp.where(
        flat,
        -high,
        jnp.where(quarter == 2, -pltpu.roll(mid, 7, 0), jnp.where(quarter == 1, -pltpu.roll(low, 6, 0), 0.0)),
    )
    high = jnp.where(flat, -1.0, high)
    mid = jnp.where(flat, 0.0, mid)
    low = jnp.where(flat, 0.0, low)
    return [high, mid, high, mid, low, high, own, jnp.zeros_like(z)]


def masked(groups, half):
    keep = (rows_of(groups[0].shape[1]) >> 2) == half
    return jnp.concatenate([jnp.where(keep, g, 0.0) for g in groups], axis=0).astype(BF16)


def weighted_sum(weighted, weight, pieces, flip):
    dims = (((1,), (1 if flip else 0,)), ((), ()))
    high = weight.astype(BF16)
    total = lax.dot_general(weighted, high, dims, preferred_element_type=F32)
    if pieces == 2:
        rest = (weight - high.astype(F32)).astype(BF16)
        total = total + lax.dot_general(weighted, rest, dims, preferred_element_type=F32)
    return total[:8] + total[8:]


def block_items(sources, weighted, targets, t, kind, others=None):
    items = []
    for h in range(2):
        rows = slice(h * HALF, (h + 1) * HALF)
        width = HALF if kind == "self" and h == 0 else PA
        flips = None
        if kind == "self" and h == 1:
            flips = (weighted, HALF, (t, 1))
        if kind == "cross":
            flips = (others, PA, (1, h))
        items.append((sources, rows, weighted, targets, width, t, flips))
    return items


def run_items(items, pieces):
    waiting = None
    for item, sums_of in list(items) + [(None, None)]:
        exponent = None
        if item is not None:
            sources, rows, _, targets, width = item[:5]
            exponent = jnp.dot(sources[rows, :], targets[:, :width], preferred_element_type=F32)
        if waiting is not None:
            (_, rows, weighted, _, width, t, flips), held, sums = waiting
            weight = jnp.exp2(held)
            direct = weighted_sum(weighted[:, rows], weight, pieces, False)
            for half in range(width // HALF):
                part = direct[:, half * HALF:(half + 1) * HALF]
                sums[t, half] = sums[t, half] + part if (t, half) in sums else part
            if flips is not None:
                shares, depth, key = flips
                part = weighted_sum(shares[:, :depth], weight[:, :depth], pieces, True)
                sums[key] = sums[key] + part if key in sums else part
        waiting = (item, exponent, sums_of)


def forces_of(z, sums):
    quarter = rows_of(z.shape[1]) & 3
    plain = jnp.where(quarter == 3, sums, 0.0)
    spread = pltpu.roll(plain, 7, 0) + pltpu.roll(plain, 6, 0) + pltpu.roll(plain, 5, 0)
    return jnp.where(quarter == 3, 0.0, z * spread - sums)


def kernel(
    nb, ns, planes_total,
    table, pos, vel, mass, amp, chg,
    moved, final,
    X, V, AF, AS, prm, prm_l, prm_r, halo_l, halo_r, ring_p, ring_n,
    part_s, part_r, Y, y_l, y_r, far_s, far_r,
    nST, nXS, nT, nG, fST, fXS, fT, fG,
    prm_ss, prm_rs, halo_ss, halo_rs, ring_ss, ring_rs, part_ss, part_rs, y_ss, y_rs, far_ss, far_rs,
):
    me_b = lax.axis_index("bead")
    me_s = lax.axis_index("slab")
    left = (me_b, lax.rem(me_s + ns - 1, ns))
    right = (me_b, lax.rem(me_s + 1, ns))
    prev = (lax.rem(me_b + nb - 1, nb), me_s)
    after = (lax.rem(me_b + 1, nb), me_s)
    pairs = X.shape[1]
    beads_here = 2 * pairs
    atoms = X.shape[3]
    first_bead = me_b * beads_here

    def remote(src, dst, ss, rs, to):
        return pltpu.make_async_remote_copy(
            src_ref=src, dst_ref=dst, send_sem=ss, recv_sem=rs, device_id=to, device_id_type=MESH
        )

    barrier = pltpu.get_barrier_semaphore()
    pl.semaphore_signal(barrier, inc=1, device_id=left, device_id_type=MESH)
    pl.semaphore_signal(barrier, inc=1, device_id=right, device_id_type=MESH)
    for d in range(1, nb):
        other = (lax.rem(me_b + d, nb), me_s)
        pl.semaphore_signal(barrier, inc=1, device_id=other, device_id_type=MESH)

    X[0] = jnp.zeros((pairs, 8, atoms), F32)
    V[...] = jnp.zeros_like(V)
    for b in range(beads_here):
        p, r = b // 2, 4 * (b % 2)
        for c in range(3):
            X[0, p, r + c:r + c + 1, :] = pos[c, b:b + 1, :]
            V[p, r + c:r + c + 1, :] = vel[c, b:b + 1, :]
    prm[...] = jnp.zeros_like(prm)
    for t in range(2):
        lanes = slice(t * PA, (t + 1) * PA)
        prm[t:t + 1, :] = amp[:, lanes]
        prm[2 + t:3 + t, :] = chg[:, lanes]

    pl.semaphore_wait(barrier, nb + 1)

    prm_copies = [
        remote(prm, prm_r, prm_ss.at[0], prm_rs.at[0], left),
        remote(prm, prm_l, prm_ss.at[1], prm_rs.at[1], right),
    ]
    for copy in prm_copies:
        copy.start()

    centre = (me_s * 2).astype(F32) + 1.0
    span = float(planes_total)
    centre_l = centre + jnp.where(me_s == 0, span, 0.0)
    centre_r = centre - jnp.where(me_s == ns - 1, span, 0.0)
    near_rate = math.sqrt(near_scale / math.log(2.0))
    far_rate = math.sqrt(far_scale / math.log(2.0))

    inverse = 1.0 / mass[...]

    def halo_copies(k):
        return [
            remote(X.at[k, :, :, pl.ds(0, PA)], halo_r.at[k], halo_ss.at[k, 0], halo_rs.at[k, 0], left),
            remote(X.at[k, :, :, pl.ds(atoms - PA, PA)], halo_l.at[k], halo_ss.at[k, 1], halo_rs.at[k, 1], right),
        ]

    def ring_copies(k):
        return [
            remote(X.at[k, pairs - 1], ring_p.at[k], ring_ss.at[k, 0], ring_rs.at[k, 0], after),
            remote(X.at[k, 0], ring_n.at[k], ring_ss.at[k, 1], ring_rs.at[k, 1], prev),
        ]

    def spoke_copies(src, dst, ss, rs, e):
        return [
            remote(src(d), dst.at[e, d], ss.at[e, d], rs.at[e, d], (lax.rem(me_b + d, nb), me_s))
            for d in range(1, nb)
        ]

    def part_copies(e):
        return spoke_copies(lambda d: part_s.at[e, d], part_r, part_ss, part_rs, e)

    def far_copies(e):
        return spoke_copies(lambda d: far_s.at[e], far_r, far_ss, far_rs, e)

    def y_copies(e):
        return [
            remote(Y.at[e], y_r.at[e], y_ss.at[e, 0], y_rs.at[e, 0], left),
            remote(Y.at[e], y_l.at[e], y_ss.at[e, 1], y_rs.at[e, 1], right),
        ]

    low_rows = rows_of(PA) < 4

    def partial_of(k, c):
        total = None
        for p in range(pairs):
            first = table[c, first_bead + 2 * p]
            second = table[c, first_bead + 2 * p + 1]
            term = jnp.where(rows_of(atoms) < 4, first, second) * X[k, p]
            total = term if total is None else total + term
        total = total + pltpu.roll(total, 4, 0)
        return jnp.where(low_rows, total[:, :PA], total[:, PA:])

    def far_halves(tile):
        first = jnp.where(low_rows, tile, 0.0)
        second = jnp.where(low_rows, pltpu.roll(tile, 4, 0), 0.0)
        return first, second

    def near_items(p, part, blocks):
        items = []
        for t, q, kind in blocks:
            others = nXS.at[p, 1] if kind == "cross" else None
            items += block_items(nST.at[p, q], nXS.at[p, q], nT.at[p, t, part], t, kind, others)
        return items

    def near_blocks(p, blocks, first):
        sums = ({}, {})
        run_items([(item, sums[part]) for part in range(2) for item in near_items(p, part, blocks)], 1)
        for t, half in sums[0]:
            lanes = slice(half * HALF, (half + 1) * HALF)
            both = jnp.where(rows_of(HALF) < 4, sums[0][t, half], sums[1][t, half])
            if first:
                nG[p, t, :, lanes] = both
            else:
                nG[p, t, :, lanes] += both

    def far_blocks(blocks, first):
        items, sums = [], {}
        for t, q, kind in blocks:
            others = fXS.at[2] if kind == "cross" else None
            items += block_items(fST.at[q], fXS.at[q], fT.at[t], t, kind, others)
        run_items([(item, sums) for item in items], 2)
        for t, half in sums:
            lanes = slice(half * HALF, (half + 1) * HALF)
            if first:
                fG[t, :, lanes] = sums[t, half]
            else:
                fG[t, :, lanes] += sums[t, half]

    near_own = ((0, 1, "self"), (0, 2, "cross"), (1, 2, "self"))
    near_rim = ((0, 0, "rim"), (1, 3, "rim"))
    far_own = ((0, 2, "self"), (0, 3, "cross"), (1, 3, "self"))
    far_rim = ((0, 0, "rim"), (0, 1, "rim"), (0, 4, "rim"), (1, 1, "rim"), (1, 4, "rim"), (1, 5, "rim"))

    def phase(k, carry):
        slow_turn = lax.rem(k, INNER_STEPS) == 0
        e = k // INNER_STEPS
        for copy in halo_copies(k):
            copy.start()

        @pl.when(slow_turn)
        def _():
            for d in range(1, nb):
                part_s[e, d] = partial_of(k, lax.rem(me_b + d, nb))
            for copy in part_copies(e):
                copy.start()

        for copy in ring_copies(k):
            copy.start()

        for p in range(pairs):
            for t in range(2):
                lanes = slice(t * PA, (t + 1) * PA)
                z = scaled(X[k, p, :, lanes], centre, near_rate)
                nST[p, 1 + t], nXS[p, 1 + t] = source_features(z, amp[:, lanes])
                groups = target_features(z)
                nT[p, t, 0] = masked(groups, 0)
                nT[p, t, 1] = masked(groups, 1)

        @pl.loop(0, pairs // 2)
        def _(p):
            near_blocks(p, near_own, True)

        @pl.when(slow_turn)
        def _():
            total = partial_of(k, me_b)
            for d, copy in enumerate(part_copies(e)):
                copy.wait_recv()
                total = total + part_r[e, d + 1]
            Y[e] = total
            for copy in y_copies(e):
                copy.start()

        @pl.loop(pairs // 2, pairs)
        def _(p):
            near_blocks(p, near_own, True)

        @pl.when(slow_turn)
        def _():
            for t, half in enumerate(far_halves(Y[e])):
                z = scaled(half, centre, far_rate)
                z = jnp.where(low_rows, z, 0.0)
                fST[2 + t], fXS[2 + t] = source_features(z, chg[:, t * PA:(t + 1) * PA])
                fT[t] = masked(target_features(z), 0)
            far_blocks(far_own, True)

        @pl.when(k == 0)
        def _():
            for copy in prm_copies:
                copy.wait_recv()

        for copy in halo_copies(k):
            copy.wait_recv()
        for p in range(pairs):
            z = scaled(halo_l[k, p], centre_l, near_rate)
            nST[p, 0], nXS[p, 0] = source_features(z, prm_l[1:2, :])
            z = scaled(halo_r[k, p], centre_r, near_rate)
            nST[p, 3], nXS[p, 3] = source_features(z, prm_r[0:1, :])

        @pl.loop(0, pairs // 2)
        def _(p):
            near_blocks(p, near_rim, False)

        @pl.when(slow_turn)
        def _():
            for copy in y_copies(e):
                copy.wait_recv()
            for base, tile, shares, middle in ((0, y_l, prm_l, centre_l), (4, y_r, prm_r, centre_r)):
                for t, half in enumerate(far_halves(tile[e])):
                    z = scaled(half, middle, far_rate)
                    z = jnp.where(low_rows, z, 0.0)
                    fST[base + t], fXS[base + t] = source_features(z, shares[2 + t:3 + t, :])
            far_blocks(far_rim, False)
            halves = []
            for t, half in enumerate(far_halves(Y[e])):
                lanes = slice(t * PA, (t + 1) * PA)
                z = scaled(half, centre, far_rate)
                coefficient = chg[:, lanes] * (far_scale / far_rate)
                halves.append(coefficient * forces_of(z, fG[t]))
            far_s[e] = jnp.where(low_rows, halves[0], pltpu.roll(halves[1], 4, 0))
            for copy in far_copies(e):
                copy.start()

        @pl.loop(pairs // 2, pairs)
        def _(p):
            near_blocks(p, near_rim, False)

        for copy in ring_copies(k):
            copy.wait_recv()
        upper = rows_of(atoms) < 4
        rolled = [pltpu.roll(X[k, p], 4, 0) for p in range(pairs)]
        before = [pltpu.roll(ring_p[k], 4, 0)] + rolled
        behind = rolled + [pltpu.roll(ring_n[k], 4, 0)]
        for p in range(pairs):
            springs = 2.0 * X[k, p] - rolled[p] - jnp.where(upper, before[p], behind[p + 1])
            AF[p] = -spring_rate * springs
            for t in range(2):
                lanes = slice(t * PA, (t + 1) * PA)
                z = scaled(X[k, p, :, lanes], centre, near_rate)
                coefficient = amp[:, lanes] * (near_scale / near_rate) * inverse[:, lanes]
                AF[p, :, lanes] += coefficient * forces_of(z, nG[p, t])

        edge = (k == 0) | (k == PHASES - 1)
        fast_step = jnp.where(edge, 0.5 * time_step, time_step)
        slow_step = jnp.where(edge, 0.5 * INNER_STEPS * time_step, INNER_STEPS * time_step)
        for p in range(pairs):
            V[p] += fast_step * AF[p]

        @pl.when(slow_turn)
        def _():
            for copy in far_copies(e):
                copy.wait_recv()
            ratio = float(beads_here)
            total = [[None, None] for _ in range(pairs)]
            for d in range(nb):
                tile = far_s[e] if d == 0 else far_r[e, d]
                c = lax.rem(me_b + nb - d, nb)
                turned = pltpu.roll(tile, 4, 0)
                doubled = (jnp.where(low_rows, tile, turned), jnp.where(low_rows, turned, tile))
                for p in range(pairs):
                    first = table[c, first_bead + 2 * p] * ratio
                    second = table[c, first_bead + 2 * p + 1] * ratio
                    level = jnp.where(low_rows, first, second)
                    for t in range(2):
                        term = level * doubled[t]
                        total[p][t] = term if d == 0 else total[p][t] + term
            for p in range(pairs):
                for t in range(2):
                    lanes = slice(t * PA, (t + 1) * PA)
                    V[p, :, lanes] += slow_step * inverse[:, lanes] * total[p][t]

        @pl.when(k < PHASES - 1)
        def _():
            for p in range(pairs):
                X[k + 1, p] = X[k, p] + time_step * V[p]

        return carry

    lax.fori_loop(0, PHASES, phase, 0)

    last = PHASES - 1
    for b in range(beads_here):
        p, r = b // 2, 4 * (b % 2)
        for c in range(3):
            moved[c, b:b + 1, :] = X[last, p, r + c:r + c + 1, :] - pos[c, b:b + 1, :]
            final[c, b:b + 1, :] = V[p, r + c:r + c + 1, :]

    for copy in prm_copies:
        copy.wait_send()

    @pl.loop(0, PHASES)
    def _(k):
        for copy in halo_copies(k) + ring_copies(k):
            copy.wait_send()

    @pl.loop(0, EVENTS)
    def _(e):
        for copy in part_copies(e) + y_copies(e) + far_copies(e):
            copy.wait_send()


def solution(mesh):
    nb, ns = mesh.shape["bead"], mesh.shape["slab"]

    def shards(positions, velocities, masses, amplitudes, charges):
        beads_here, _, atoms = positions.shape
        assert atoms == 2 * PA and beads_here % 2 == 0
        pairs = beads_here // 2
        table = jnp.asarray(contraction(beads_here * nb, nb))
        vmem = pl.BlockSpec(memory_space=pltpu.VMEM)
        out = jax.ShapeDtypeStruct((3, beads_here, atoms), F32)
        V, D = pltpu.VMEM, pltpu.SemaphoreType.DMA
        tile = (8, PA)

        def body(*refs):
            kernel(nb, ns, 2 * ns, *refs)

        shifted, speeds = pl.pallas_call(
            body,
            name="rod",
            out_shape=(out, out),
            in_specs=[pl.BlockSpec(memory_space=pltpu.SMEM)] + [vmem] * 5,
            out_specs=(vmem, vmem),
            scratch_shapes=[
                V((PHASES, pairs, 8, atoms), F32),
                V((pairs, 8, atoms), F32),
                V((pairs, 8, atoms), F32),
                V((pairs, 8, atoms), F32),
                V(tile, F32), V(tile, F32), V(tile, F32),
                V((PHASES, pairs) + tile, F32), V((PHASES, pairs) + tile, F32),
                V((PHASES, 8, atoms), F32), V((PHASES, 8, atoms), F32),
                V((EVENTS, nb) + tile, F32), V((EVENTS, nb) + tile, F32),
                V((EVENTS,) + tile, F32), V((EVENTS,) + tile, F32), V((EVENTS,) + tile, F32),
                V((EVENTS,) + tile, F32), V((EVENTS, nb) + tile, F32),
                V((pairs, 4, PA, FEATURES), BF16), V((pairs, 4, 16, PA), BF16),
                V((pairs, 2, 2, FEATURES, PA), BF16), V((pairs, 2) + tile, F32),
                V((6, PA, FEATURES), BF16), V((6, 16, PA), BF16),
                V((2, FEATURES, PA), BF16), V((2,) + tile, F32),
                D((2,)), D((2,)), D((PHASES, 2)), D((PHASES, 2)), D((PHASES, 2)), D((PHASES, 2)),
                D((EVENTS, nb)), D((EVENTS, nb)), D((EVENTS, 2)), D((EVENTS, 2)),
                D((EVENTS, nb)), D((EVENTS, nb)),
            ],
            compiler_params=pltpu.CompilerParams(collective_id=0, has_side_effects=True),
        )(table, positions.transpose(1, 0, 2), velocities.transpose(1, 0, 2), masses[None], amplitudes[None], charges[None])
        return shifted.transpose(1, 0, 2), speeds.transpose(1, 0, 2)

    both = P("bead", None, "slab")
    return jax.shard_map(
        shards, mesh=mesh, in_specs=(both, both, P("slab"), P("slab"), P("slab")), out_specs=(both, both), check_vma=False
    )
```
